32 devices in a mesh: seq: 16 (over z, y, x), tensor: 2 (over core).
Axes of the slice: x: 2, y: 2, z: 4, core: 2. Of those that a mesh axis runs over, the one named last changes fastest.
Arguments:
- tokens: bfloat16 [1024, 4096], P('seq', 'tensor'), may hold values from -6 to 6
- w_gate: bfloat16 [16, 4096, 4096], P('seq', None, 'tensor'), may hold values from -0.09375 to 0.09375
- w_up: bfloat16 [16, 4096, 4096], P('seq', None, 'tensor'), may hold values from -0.09375 to 0.09375
- w_down: bfloat16 [16, 4096, 4096], P('seq', None, 'tensor'), may hold values from -0.0625 to 0.0625
- routes: int32 [8, 2], replicated, may hold values from 0 to 7, all different within a row; in each aligned block of 8 rows (0 to 7, 8 to 15, ...) at most 3 rows name the same one
- gate_values: float32 [8, 2], replicated, may hold values from 0.1 to 0.9
Outputs:
- moe_out: bfloat16 [1024, 4096], P('seq', 'tensor')
The draws below stay inside these ranges and needn't reach their ends.
Inputs may be any that keep to these rules, and one draw needn't show every extreme that they name: `routes`: the two experts of a block differ; every expert is named by some block and by at most 3 blocks, and one by exactly 3.
All inputs are finite; a program needn't handle non-finite values.
Results may differ from the reference program's by a relative error of at most 0.005.
Values may be sent and summed in bfloat16 or wider, within the bound.
No kernel may reach another device: no remote copies, remote signals or barrier semaphores. Data moves between devices by JAX's collectives and lax.ppermute only.
A program may use at most 128 MiB of HBM per device.

```python
import math
import jax
import jax.numpy as jnp
import numpy as np

D = 4096
E = 8
FF = 8192
TOP = 2
BLOCK = 128
TOKENS = 1024
BLOCKS = 8
LMAX = 3
PARTS_SIZE = 2
N_SEQ = 16


def steps_of(rng, shape, pieces, smallest, high):
    level = 1.0
    for axis_at, parts in pieces:
        heights = jax.random.uniform(jax.random.fold_in(jax.random.fold_in(rng, 6), axis_at), (parts,), jnp.float32, smallest / len(pieces), high / len(pieces))
        level = level * jnp.repeat(jnp.exp(heights), shape[axis_at] // parts).reshape((-1,) + (1,) * (len(shape) - 1 - axis_at))
    return level


def assign_block(rng, own, number, rows, number_of, top, bound, skew):
    sequence = jax.random.permutation(rng, number_of)
    heavy_load, common = load_shares(number_of, rows * top, bound, skew, True), load_shares(number_of, rows * top, bound, skew, False)
    places = jnp.arange(number_of)

    def named(sizes, offset_by):
        used = int((sizes > 0).sum())
        fixed = max(1, used // 4)
        moved = fixed + (places - fixed + offset_by * (used - fixed)) % max(1, number_of - fixed)
        return jnp.zeros((number_of,), jnp.int32).at[sequence[jnp.where(places < fixed, places, moved)]].set(jnp.asarray(sizes, jnp.int32))

    sizes = jnp.where(number % 4 == 0, named(heavy_load, number // 4), named(common, number - number // 4 - 1))
    mixed = jax.random.permutation(jax.random.fold_in(own, 3), number_of)
    giver, sink = mixed[0:number_of // 2 * 2:2], mixed[1:number_of // 2 * 2:2]
    room = jnp.minimum(sizes[giver] - 1, bound - sizes[sink]) // 2
    room = jnp.where((giver == sequence[0]) | (sink == sequence[0]) | (sizes[sink] == 0), 0, jnp.maximum(room, 0))
    moved = jax.random.randint(jax.random.fold_in(own, 4), (number_of // 2,), 0, 1 << 20) % (room + 1)
    sizes = sizes.at[giver].add(-moved).at[sink].add(moved)
    members = jnp.searchsorted(jnp.cumsum(sizes), jnp.arange(rows * top), side="right").astype(jnp.int32)
    grid = members.reshape(top, rows).T
    grid = grid[jax.random.permutation(jax.random.fold_in(own, 1), rows)]
    offset_by = jax.random.randint(jax.random.fold_in(own, 2), (rows, 1), 0, top)
    return jnp.take_along_axis(grid, (jnp.arange(top)[None, :] + offset_by) % top, axis=1)


def load_shares(count, total, bound, lean, full):
    weights = [(1 << 20) // math.isqrt(rank ** lean) + 1 for rank in range(1, count + 1)]
    largest = bound if full else min(bound, max(-(-total // count), total * weights[0] // sum(weights)))
    least = 1 if total - largest >= count - 1 else 0
    given, surplus = [largest] + [least] * (count - 1), total - largest - least * (count - 1)
    while surplus > 0:
        movable = [i for i in range(1, count) if given[i] < largest] or [i for i in range(1, count) if given[i] < bound]
        mass, remaining = sum([weights[i] for i in movable]), surplus
        for i in movable:
            more = min(bound - given[i], max(1, remaining * weights[i] // mass), surplus)
            given[i] = given[i] + more
            surplus = surplus - more
    return np.array(given)


def bell_draw(stream_key, extent, deviation, reach, split=(), held_as=jnp.bfloat16):
    values = deviation * jax.random.normal(stream_key, extent, jnp.float32)
    if split:
        values = values * steps_of(stream_key, extent, split, -0.22, 0.18)
    return jnp.clip(values, -reach, reach).astype(held_as)


def setup_inputs(seed: int = 0) -> dict:
    key_list = jax.random.split(jax.random.key(seed), 7)
    tokens = bell_draw(key_list[0], (TOKENS, D), 1.0, 6.0, ((0, 16), (1, 2)))
    w_gate = bell_draw(key_list[1], (N_SEQ, D, FF // PARTS_SIZE), D ** -0.5, 0.09375, ((0, 16), (2, 2)))
    w_up = bell_draw(key_list[2], (N_SEQ, D, FF // PARTS_SIZE), D ** -0.5, 0.09375, ((0, 16), (2, 2)))
    w_down = bell_draw(key_list[3], (N_SEQ, FF // PARTS_SIZE, D), FF ** -0.5, 0.0625, ((0, 16), (2, 2)))
    routes_keys = jax.random.split(jax.random.fold_in(key_list[4], 1), BLOCKS // BLOCKS)
    routes_turns = jax.random.permutation(jax.random.fold_in(key_list[4], 3), BLOCKS // BLOCKS)
    routes = jax.vmap(lambda own, number: assign_block(jax.random.fold_in(key_list[4], 2), own, number, BLOCKS, E, TOP, LMAX, 2))(routes_keys, routes_turns).reshape((BLOCKS, TOP))
    gate_values = jnp.clip(jax.random.uniform(key_list[5], (BLOCKS, TOP), jnp.float32, 0.1, 0.9), 0.1, 0.9)
    return {"tokens": tokens, "w_gate": w_gate, "w_up": w_up, "w_down": w_down, "routes": routes, "gate_values": gate_values}


def route_slots(routes, gate_values, expert, capacity):
    block_count = routes.shape[0]
    matches = routes == expert
    member = jnp.any(matches, axis=1).astype(jnp.int32)
    weight = jnp.sum(jnp.where(matches, gate_values, 0.0), axis=1)
    position = jnp.cumsum(member) - 1
    slot_ids = jnp.arange(capacity, dtype=jnp.int32)
    picked = (member[None, :] == 1) & (position[None, :] == slot_ids[:, None])
    block_ids = jnp.arange(block_count, dtype=jnp.int32)
    block_index = jnp.sum(jnp.where(picked, block_ids[None, :], 0), axis=1).astype(jnp.int32)
    slot_gate = jnp.sum(jnp.where(picked, weight[None, :], 0.0), axis=1)
    return picked, block_index, slot_gate


def reference(tokens, w_gate, w_up, w_down, routes, gate_values):
    block_count = routes.shape[0]
    capacity = LMAX
    blocks = tokens.reshape(block_count, BLOCK, D)
    accumulated = jnp.zeros((block_count, BLOCK, D), jnp.float32)
    for expert in range(E):
        picked, block_index, slot_gate = route_slots(routes, gate_values, expert, capacity)
        expert_rows = blocks[block_index].reshape(capacity * BLOCK, D)
        gate_matrix = jnp.transpose(w_gate[expert * PARTS_SIZE:(expert + 1) * PARTS_SIZE], (1, 0, 2)).reshape(D, FF)
        up_matrix = jnp.transpose(w_up[expert * PARTS_SIZE:(expert + 1) * PARTS_SIZE], (1, 0, 2)).reshape(D, FF)
        down_matrix = w_down[expert * PARTS_SIZE:(expert + 1) * PARTS_SIZE].reshape(FF, D)
        gate_sum = jnp.dot(expert_rows, gate_matrix, preferred_element_type=jnp.float32)
        up_sum = jnp.dot(expert_rows, up_matrix, preferred_element_type=jnp.float32)
        hidden = (jax.nn.silu(gate_sum) * up_sum).astype(jnp.bfloat16)
        expert_part = jnp.dot(hidden, down_matrix, preferred_element_type=jnp.float32)
        expert_part = expert_part.reshape(capacity, BLOCK, D)
        accumulated = accumulated.at[block_index].add(expert_part * slot_gate[:, None, None])
    return accumulated.reshape(TOKENS, D).astype(jnp.bfloat16)
```

```python
import jax
import jax.numpy as jnp
from jax import lax
from jax.experimental import pallas as pl
from jax.experimental.pallas import tpu as pltpu
from jax.sharding import PartitionSpec as P


E = 8
BF16 = jnp.bfloat16
F32 = jnp.float32
D_CHUNKS = 2
C_CHUNKS = 2


def route_slots(routes, gate_values, expert, capacity):
    block_count = routes.shape[0]
    matches = routes == expert
    member = jnp.any(matches, axis=1).astype(jnp.int32)
    weight = jnp.sum(jnp.where(matches, gate_values, 0.0), axis=1)
    position = jnp.cumsum(member) - 1
    slot_ids = jnp.arange(capacity, dtype=jnp.int32)
    picked = (member[None, :] == 1) & (position[None, :] == slot_ids[:, None])
    block_ids = jnp.arange(block_count, dtype=jnp.int32)
    block_index = jnp.sum(jnp.where(picked, block_ids[None, :], 0), axis=1)
    slot_gate = jnp.sum(jnp.where(picked, weight[None, :], 0.0), axis=1)
    return (picked, block_index, slot_gate)


def gathered(tokens, w_gate, w_up, w_down, routes, gate_values):
    seq_count = lax.axis_size("seq")
    part_count = seq_count // E
    expert = lax.axis_index("seq") // part_count
    block_count = routes.shape[0]
    capacity = 3 * block_count // 8
    columns = lax.all_gather(tokens, "seq", axis=0, tiled=True)
    block_rows = columns.shape[0] // block_count
    feature_width = columns.shape[1]
    picked, block_index, slot_gate = route_slots(routes, gate_values, expert, capacity)
    chosen = columns.reshape(block_count, block_rows, feature_width)[block_index]
    chosen = chosen.reshape(capacity * block_rows, feature_width)
    full_rows = lax.all_gather(chosen, "tensor", axis=1, tiled=True)
    gate_sum = jnp.dot(full_rows, w_gate[0], preferred_element_type=F32)
    up_sum = jnp.dot(full_rows, w_up[0], preferred_element_type=F32)
    hidden = (jax.nn.silu(gate_sum) * up_sum).astype(BF16)
    quarter = lax.all_gather(hidden, "tensor", axis=1, tiled=True)
    partial_value = jnp.dot(quarter, w_down[0], preferred_element_type=F32)
    weighted = partial_value.reshape(capacity, block_rows, feature_width) * slot_gate[:, None, None]
    scattered = jnp.einsum(
        "lb,lrd->brd", picked.astype(F32), weighted, precision=lax.Precision.HIGHEST
    )
    scattered = scattered.reshape(block_count * block_rows, feature_width)
    summed = lax.psum_scatter(scattered, "seq", scatter_dimension=0, tiled=True)
    return summed.astype(BF16)


def params(mebibytes=4):
    return pltpu.CompilerParams(vmem_limit_bytes=mebibytes << 20)


def tables(routes, gate_values, lines, pairs, halves, capacity):
    block_count = routes.shape[0]
    size = 2 * capacity + 2 * lines + 1

    def kernel(routes_ref, values_ref, place_ref, gate_ref):
        me = lax.axis_index("seq")
        expert = me // halves
        z, y = expert // pairs, expert % pairs
        for l in range(capacity):
            place_ref[l] = 0
            place_ref[capacity + l] = 0
            gate_ref[l] = 0.0
        for k in range(2 * lines):
            place_ref[2 * capacity + k] = capacity
        place_ref[size - 1] = lax.axis_index("tensor")
        for side in range(2):
            wanted = expert if side == 0 else expert ^ 1
            count = jnp.int32(0)
            for b in range(block_count):
                first, second = routes_ref[b, 0] == wanted, routes_ref[b, 1] == wanted
                named = jnp.logical_or(first, second)
                here = y == b % pairs
                place = (z - b // pairs + lines) % lines
                slot = jnp.minimum(count, capacity - 1)

                @pl.when(named)
                def _():
                    if side == 0:
                        place_ref[slot] = jnp.where(here, place, lines)
                        gate_ref[slot] = jnp.where(first, values_ref[b, 0], values_ref[b, 1])
                    else:
                        place_ref[capacity + slot] = place

                    @pl.when(here)
                    def _():
                        place_ref[2 * capacity + 2 * ((lines - place) % lines) + side] = slot

                count = count + named.astype(jnp.int32)

    scalar = pl.BlockSpec(memory_space=pltpu.SMEM)
    return pl.pallas_call(
        kernel,
        out_shape=[
            jax.ShapeDtypeStruct((size,), jnp.int32),
            jax.ShapeDtypeStruct((capacity,), F32),
        ],
        in_specs=[scalar, scalar],
        out_specs=[scalar, scalar],
        compiler_params=params(),
    )(routes, gate_values)


INSIDE = pl.BlockSpec(memory_space=pltpu.VMEM)
SCALAR = pl.BlockSpec(memory_space=pltpu.SMEM)


def pick(sources, places, first, capacity, rows, came=None):
    width = sources[0].shape[1]
    extra = [] if came is None else [came]

    def kernel(place_ref, *refs):
        out_ref = refs[-1]
        for l in range(capacity):
            here = pl.ds(l * rows, rows)
            for s, ref in enumerate(refs[: len(sources)]):

                @pl.when(place_ref[first + l] == s)
                def _():
                    out_ref[here, :] = ref[...]

            if came is not None:

                @pl.when(place_ref[first + l] == len(sources))
                def _():
                    out_ref[here, :] = refs[len(sources)][here, :]

    size = capacity * rows * width
    return pl.pallas_call(
        kernel,
        out_shape=jax.ShapeDtypeStruct((capacity * rows, width), BF16),
        in_specs=[SCALAR] + [INSIDE] * (len(sources) + len(extra)),
        out_specs=INSIDE,
        cost_estimate=pl.CostEstimate(flops=size, bytes_accessed=6 * size, transcendentals=0),
        compiler_params=params(),
    )(places, *sources, *extra)


def gate_up(pieces, w_gate, w_up, places, chunk, tile, sums=()):
    half, step = pieces[0].shape
    rows = 2 * half
    depth, width = w_gate.shape
    per_side = depth // 2 // step
    final = chunk == per_side - 1
    last = places.shape[0] - 1
    count = len(sums)

    def kernel(place_ref, own_ref, far_ref, mate_ref, mate_far_ref, g0, g1, u0, u1, *refs):
        sum_refs, out_refs, x_ref = refs[:count], refs[count:-1], refs[-1]

        @pl.when(pl.program_id(0) == 0)
        def _():
            x_ref[:half, :step] = own_ref[...]
            x_ref[:half, step:] = far_ref[...]
            x_ref[half:, :step] = mate_ref[...]
            x_ref[half:, step:] = mate_far_ref[...]

        def dot(ref0, ref1):
            return jnp.dot(
                x_ref[:, :step], ref0[...], preferred_element_type=F32
            ) + jnp.dot(x_ref[:, step:], ref1[...], preferred_element_type=F32)

        gate, up = dot(g0, g1), dot(u0, u1)
        if sum_refs:
            gate, up = gate + sum_refs[0][...], up + sum_refs[1][...]
        if final:
            out_refs[0][...] = (gate / (1.0 + jnp.exp(-gate)) * up).astype(BF16)
        else:
            out_refs[0][...], out_refs[1][...] = gate, up

    near_rows = pl.BlockSpec((step, tile), lambda i, p: (p[last] * per_side + chunk, i))
    far_rows = pl.BlockSpec((step, tile), lambda i, p: ((1 - p[last]) * per_side + chunk, i))
    column = pl.BlockSpec((rows, tile), lambda i, p: (0, i))
    wide = jax.ShapeDtypeStruct((rows, width), F32)
    return pl.pallas_call(
        kernel,
        out_shape=jax.ShapeDtypeStruct((rows, width), BF16) if final else [wide, wide],
        grid_spec=pltpu.PrefetchScalarGridSpec(
            num_scalar_prefetch=1,
            grid=(width // tile,),
            in_specs=[pl.BlockSpec(a.shape, lambda i, p: (0, 0)) for a in pieces]
            + [near_rows, far_rows, near_rows, far_rows]
            + [column] * count,
            out_specs=column if final else [column, column],
            scratch_shapes=[pltpu.VMEM((rows, 2 * step), BF16)],
        ),
        cost_estimate=pl.CostEstimate(
            flops=8 * rows * step * width,
            bytes_accessed=8 * step * width + 4 * rows * step + 8 * rows * width,
            transcendentals=rows * width if final else 0,
        ),
        compiler_params=params(44),
    )(places, *pieces, w_gate, w_gate, w_up, w_up, *sums)


def down(hidden, far, w_down, places, gates, tile, first, width):
    streamed = w_down.shape[1] > width
    rows, half = hidden.shape
    capacity = gates.shape[0]
    part = rows // 2 // capacity

    def kernel(place_ref, gate_ref, own_ref, far_ref, w_ref, keep_ref, send_ref):
        core = place_ref[places.shape[0] - 1]
        here = pl.multiple_of(core * half, half)
        there = pl.multiple_of((1 - core) * half, half)
        for i in range(1 if streamed else width // tile):
            columns = slice(i * tile, (i + 1) * tile)
            total = jnp.dot(
                own_ref[...], w_ref[pl.ds(here, half), columns], preferred_element_type=F32
            ) + jnp.dot(
                far_ref[...], w_ref[pl.ds(there, half), columns], preferred_element_type=F32
            )
            for l in range(capacity):
                mine = slice(l * part, (l + 1) * part)
                other = slice(rows // 2 + l * part, rows // 2 + (l + 1) * part)
                keep_ref[mine, columns] = total[mine] * gate_ref[l]
                send_ref[mine, columns] = (total[other] * gate_ref[l]).astype(BF16)

    if streamed:
        resident = pl.BlockSpec((rows, half), lambda i: (0, 0))
        column = pl.BlockSpec((rows // 2, tile), lambda i: (0, i))
        specs = {
            "grid": (width // tile,),
            "in_specs": [SCALAR, SCALAR, resident, resident]
            + [pl.BlockSpec((2 * half, tile), lambda i: (0, i + first // tile))],
            "out_specs": [column, column],
            "compiler_params": params(44),
        }
    else:
        specs = {
            "in_specs": [SCALAR, SCALAR, INSIDE, INSIDE, INSIDE],
            "out_specs": [INSIDE, INSIDE],
            "compiler_params": params(),
        }
    return pl.pallas_call(
        kernel,
        out_shape=[
            jax.ShapeDtypeStruct((rows // 2, width), F32),
            jax.ShapeDtypeStruct((rows // 2, width), BF16),
        ],
        cost_estimate=pl.CostEstimate(
            flops=4 * rows * half * width,
            bytes_accessed=4 * rows * half + 3 * rows * width,
            transcendentals=0,
        ),
        **specs,
    )(places, gates, hidden, far, w_down)


def join(kept, arrived):
    def kernel(kept_ref, arrived_ref, out_ref):
        out_ref[...] = (kept_ref[...] + arrived_ref[...].astype(F32)).astype(BF16)

    size = kept.shape[0] * kept.shape[1]
    return pl.pallas_call(
        kernel,
        out_shape=jax.ShapeDtypeStruct(kept.shape, BF16),
        in_specs=[INSIDE, INSIDE],
        out_specs=INSIDE,
        cost_estimate=pl.CostEstimate(flops=size, bytes_accessed=8 * size, transcendentals=0),
        compiler_params=params(),
    )(kept, arrived)


def share_out(kept, arrived, near, places, lines, rows, capacity):
    width = kept.shape[1]

    def kernel(place_ref, kept_ref, arrived_ref, near_ref, *out_refs):
        for k in range(lines):
            mine = place_ref[2 * capacity + 2 * k]
            other = place_ref[2 * capacity + 2 * k + 1]
            start = pl.multiple_of(jnp.minimum(mine, capacity - 1) * rows, rows)
            value = kept_ref[pl.ds(start, rows), :] + arrived_ref[pl.ds(start, rows), :].astype(F32)
            value = jnp.where(mine < capacity, value, 0.0)
            start = pl.multiple_of(jnp.minimum(other, capacity - 1) * rows, rows)
            more = near_ref[pl.ds(start, rows), :].astype(F32)
            value = value + jnp.where(other < capacity, more, 0.0)
            out_refs[k][...] = value.astype(out_refs[k].dtype)

    size = rows * width
    kinds = [F32] + [BF16] * (lines - 1)
    return pl.pallas_call(
        kernel,
        out_shape=[jax.ShapeDtypeStruct((rows, width), kind) for kind in kinds],
        in_specs=[SCALAR, INSIDE, INSIDE, INSIDE],
        out_specs=[INSIDE] * lines,
        cost_estimate=pl.CostEstimate(
            flops=8 * size, bytes_accessed=(8 * capacity + 10) * size, transcendentals=0
        ),
        compiler_params=params(),
    )(places, kept, arrived, near)


def homed(tokens, w_gate, w_up, w_down, routes, gate_values):
    seq_count = lax.axis_size("seq")
    lines, pairs, halves = seq_count // 4, 2, 2
    capacity = 3 * routes.shape[0] // 8
    rows, width = tokens.shape

    flip_y = [(s, s ^ 2) for s in range(seq_count)]
    flip_x = [(s, s ^ 1) for s in range(seq_count)]
    swap = [(0, 1), (1, 0)]

    def along_z(k):
        return [(s, (s + 4 * k) % seq_count) for s in range(seq_count)]

    step = width // D_CHUNKS
    held = []
    for j in range(D_CHUNKS):
        chunk = tokens[:, j * step : (j + 1) * step]
        held.append([chunk] + [lax.ppermute(chunk, "seq", along_z(k)) for k in range(1, lines)])

    places, gates = tables(routes, gate_values, lines, pairs, halves, capacity)

    own = []
    for j in range(D_CHUNKS):
        leave = pick(held[j], places, capacity, capacity, rows)
        came = lax.ppermute(leave, "seq", flip_y)
        own.append(pick(held[j], places, 0, capacity, rows, came))
    mate = [lax.ppermute(a, "seq", flip_x) for a in own]
    far = [lax.ppermute(a, "tensor", swap) for a in own]
    mate_far = [lax.ppermute(a, "tensor", swap) for a in mate]

    state = ()
    for j in range(D_CHUNKS):
        pieces = (own[j], far[j], mate[j], mate_far[j])
        state = gate_up(pieces, w_gate[0], w_up[0], places, j, 256, state)
    hidden = state
    hidden_far = lax.ppermute(hidden, "tensor", swap)

    step = width // C_CHUNKS
    kept, arrived = [], []
    for j in range(C_CHUNKS):
        keep, leave = down(hidden, hidden_far, w_down[0], places, gates, 256, j * step, step)
        kept.append(keep)
        arrived.append(lax.ppermute(leave, "seq", flip_x))
    results = []
    for j in range(C_CHUNKS):
        leave = join(kept[j], arrived[j])
        near = lax.ppermute(leave, "seq", flip_y)
        outgoing = share_out(kept[j], arrived[j], near, places, lines, rows, capacity)
        result = outgoing[0]
        for k in range(1, lines):
            result = result + lax.ppermute(outgoing[k], "seq", along_z(k)).astype(F32)
        results.append(result.astype(BF16))
    return jnp.concatenate(results, axis=1)


def solution(mesh):
    placed = (
        P("seq", "tensor"),
        P("seq", None, "tensor"),
        P("seq", None, "tensor"),
        P("seq", None, "tensor"),
        P(),
        P(),
    )
    seq_count, tensor_count = mesh.shape["seq"], mesh.shape["tensor"]
    shared_home = seq_count == 2 * E and tensor_count == 2

    def per_device(*arrays):
        return homed(*arrays) if shared_home else gathered(*arrays)

    return jax.shard_map(
        per_device, mesh=mesh, in_specs=placed, out_specs=P("seq", "tensor"), check_vma=False
    )
```

```python
import jax
import jax.numpy as jnp
from jax import lax
from jax.experimental import pallas as pl
from jax.experimental.pallas import tpu as pltpu
from jax.sharding import PartitionSpec as P


E = 8
BF16 = jnp.bfloat16
F32 = jnp.float32
D_CHUNKS = 4
C_CHUNKS = 4
GROUPS = 2


def route_slots(routes, gate_values, expert, capacity):
    block_count = routes.shape[0]
    matches = routes == expert
    member = jnp.any(matches, axis=1).astype(jnp.int32)
    weight = jnp.sum(jnp.where(matches, gate_values, 0.0), axis=1)
    position = jnp.cumsum(member) - 1
    slot_ids = jnp.arange(capacity, dtype=jnp.int32)
    picked = (member[None, :] == 1) & (position[None, :] == slot_ids[:, None])
    block_ids = jnp.arange(block_count, dtype=jnp.int32)
    block_index = jnp.sum(jnp.where(picked, block_ids[None, :], 0), axis=1)
    slot_gate = jnp.sum(jnp.where(picked, weight[None, :], 0.0), axis=1)
    return (picked, block_index, slot_gate)


def gathered(tokens, w_gate, w_up, w_down, routes, gate_values):
    seq_count = lax.axis_size("seq")
    part_count = seq_count // E
    expert = lax.axis_index("seq") // part_count
    block_count = routes.shape[0]
    capacity = 3 * block_count // 8
    columns = lax.all_gather(tokens, "seq", axis=0, tiled=True)
    block_rows = columns.shape[0] // block_count
    feature_width = columns.shape[1]
    picked, block_index, slot_gate = route_slots(routes, gate_values, expert, capacity)
    chosen = columns.reshape(block_count, block_rows, feature_width)[block_index]
    chosen = chosen.reshape(capacity * block_rows, feature_width)
    full_rows = lax.all_gather(chosen, "tensor", axis=1, tiled=True)
    gate_sum = jnp.dot(full_rows, w_gate[0], preferred_element_type=F32)
    up_sum = jnp.dot(full_rows, w_up[0], preferred_element_type=F32)
    hidden = (jax.nn.silu(gate_sum) * up_sum).astype(BF16)
    quarter = lax.all_gather(hidden, "tensor", axis=1, tiled=True)
    partial_value = jnp.dot(quarter, w_down[0], preferred_element_type=F32)
    weighted = partial_value.reshape(capacity, block_rows, feature_width) * slot_gate[:, None, None]
    scattered = jnp.einsum(
        "lb,lrd->brd", picked.astype(F32), weighted, precision=lax.Precision.HIGHEST
    )
    scattered = scattered.reshape(block_count * block_rows, feature_width)
    summed = lax.psum_scatter(scattered, "seq", scatter_dimension=0, tiled=True)
    return summed.astype(BF16)


def params(mebibytes=4):
    return pltpu.CompilerParams(vmem_limit_bytes=mebibytes << 20)


def tables(routes, gate_values, lines, pairs, halves, capacity):
    block_count = routes.shape[0]
    size = 2 * capacity + 2 * lines + 1

    def kernel(routes_ref, values_ref, place_ref, gate_ref):
        me = lax.axis_index("seq")
        expert = me // halves
        z, y = expert // pairs, expert % pairs
        for l in range(capacity):
            place_ref[l] = 0
            place_ref[capacity + l] = 0
            gate_ref[l] = 0.0
        for k in range(2 * lines):
            place_ref[2 * capacity + k] = capacity
        place_ref[size - 1] = lax.axis_index("tensor")
        for side in range(2):
            wanted = expert if side == 0 else expert ^ 1
            count = jnp.int32(0)
            for b in range(block_count):
                first, second = routes_ref[b, 0] == wanted, routes_ref[b, 1] == wanted
                named = jnp.logical_or(first, second)
                here = y == b % pairs
                place = (b // pairs) ^ z
                slot = jnp.minimum(count, capacity - 1)

                @pl.when(named)
                def _():
                    if side == 0:
                        place_ref[slot] = jnp.where(here, place, lines)
                        gate_ref[slot] = jnp.where(first, values_ref[b, 0], values_ref[b, 1])
                    else:
                        place_ref[capacity + slot] = place

                    @pl.when(here)
                    def _():
                        place_ref[2 * capacity + 2 * place + side] = slot

                count = count + named.astype(jnp.int32)

    scalar = pl.BlockSpec(memory_space=pltpu.SMEM)
    return pl.pallas_call(
        kernel,
        out_shape=[
            jax.ShapeDtypeStruct((size,), jnp.int32),
            jax.ShapeDtypeStruct((capacity,), F32),
        ],
        in_specs=[scalar, scalar],
        out_specs=[scalar, scalar],
        compiler_params=params(),
    )(routes, gate_values)


INSIDE = pl.BlockSpec(memory_space=pltpu.VMEM)
SCALAR = pl.BlockSpec(memory_space=pltpu.SMEM)


def pick(sources, places, first, capacity, rows, came=None):
    width = sources[0].shape[1]
    extra = [] if came is None else [came]

    def kernel(place_ref, *refs):
        out_ref = refs[-1]
        for l in range(capacity):
            here = pl.ds(l * rows, rows)
            for s, ref in enumerate(refs[: len(sources)]):

                @pl.when(place_ref[first + l] == s)
                def _():
                    out_ref[here, :] = ref[...]

            if came is not None:

                @pl.when(place_ref[first + l] == len(sources))
                def _():
                    out_ref[here, :] = refs[len(sources)][here, :]

    size = capacity * rows * width
    return pl.pallas_call(
        kernel,
        out_shape=jax.ShapeDtypeStruct((capacity * rows, width), BF16),
        in_specs=[SCALAR] + [INSIDE] * (len(sources) + len(extra)),
        out_specs=INSIDE,
        cost_estimate=pl.CostEstimate(flops=size, bytes_accessed=6 * size, transcendentals=0),
        compiler_params=params(),
    )(places, *sources, *extra)


def gate_up(pieces, w_gate, w_up, places, chunk, tile, sums=()):
    half, part = pieces[0][0].shape
    parts = len(pieces)
    step = parts * part
    rows = 2 * half
    depth, width = w_gate.shape
    per_side = depth // 2 // step
    final = chunk == per_side - 1
    last = places.shape[0] - 1
    count = len(sums)

    def kernel(place_ref, *refs):
        piece_refs, refs = refs[: 4 * parts], refs[4 * parts :]
        g0, g1, u0, u1 = refs[:4]
        refs = refs[4:]
        sum_refs, out_refs, x_ref = refs[:count], refs[count:-1], refs[-1]

        @pl.when(pl.program_id(0) == 0)
        def _():
            for j in range(parts):
                own_ref, far_ref, mate_ref, mate_far_ref = piece_refs[4 * j : 4 * j + 4]
                near = pl.ds(j * part, part)
                beyond = pl.ds(step + j * part, part)
                x_ref[:half, near] = own_ref[...]
                x_ref[:half, beyond] = far_ref[...]
                x_ref[half:, near] = mate_ref[...]
                x_ref[half:, beyond] = mate_far_ref[...]

        def dot(ref0, ref1):
            return jnp.dot(
                x_ref[:, :step], ref0[...], preferred_element_type=F32
            ) + jnp.dot(x_ref[:, step:], ref1[...], preferred_element_type=F32)

        gate, up = dot(g0, g1), dot(u0, u1)
        if sum_refs:
            gate, up = gate + sum_refs[0][...], up + sum_refs[1][...]
        if final:
            out_refs[0][...] = (gate / (1.0 + jnp.exp(-gate)) * up).astype(BF16)
        else:
            out_refs[0][...], out_refs[1][...] = gate, up

    near_rows = pl.BlockSpec((step, tile), lambda i, p: (p[last] * per_side + chunk, i))
    far_rows = pl.BlockSpec((step, tile), lambda i, p: ((1 - p[last]) * per_side + chunk, i))
    column = pl.BlockSpec((rows, tile), lambda i, p: (0, i))
    wide = jax.ShapeDtypeStruct((rows, width), F32)
    return pl.pallas_call(
        kernel,
        out_shape=jax.ShapeDtypeStruct((rows, width), BF16) if final else [wide, wide],
        grid_spec=pltpu.PrefetchScalarGridSpec(
            num_scalar_prefetch=1,
            grid=(width // tile,),
            in_specs=[pl.BlockSpec(a.shape, lambda i, p: (0, 0)) for piece in pieces for a in piece]
            + [near_rows, far_rows, near_rows, far_rows]
            + [column] * count,
            out_specs=column if final else [column, column],
            scratch_shapes=[pltpu.VMEM((rows, 2 * step), BF16)],
        ),
        cost_estimate=pl.CostEstimate(
            flops=8 * rows * step * width,
            bytes_accessed=8 * step * width + 4 * rows * step + 8 * rows * width,
            transcendentals=rows * width if final else 0,
        ),
        compiler_params=params(44),
    )(places, *(a for piece in pieces for a in piece), w_gate, w_gate, w_up, w_up, *sums)


def down(hidden, far, w_down, places, gates, tile, first, width):
    streamed = w_down.shape[1] > width
    rows, half = hidden.shape
    capacity = gates.shape[0]
    part = rows // 2 // capacity

    def kernel(place_ref, gate_ref, own_ref, far_ref, w_ref, keep_ref, send_ref):
        core = place_ref[places.shape[0] - 1]
        here = pl.multiple_of(core * half, half)
        there = pl.multiple_of((1 - core) * half, half)
        for i in range(1 if streamed else width // tile):
            columns = slice(i * tile, (i + 1) * tile)
            total = jnp.dot(
                own_ref[...], w_ref[pl.ds(here, half), columns], preferred_element_type=F32
            ) + jnp.dot(
                far_ref[...], w_ref[pl.ds(there, half), columns], preferred_element_type=F32
            )
            for l in range(capacity):
                mine = slice(l * part, (l + 1) * part)
                other = slice(rows // 2 + l * part, rows // 2 + (l + 1) * part)
                keep_ref[mine, columns] = total[mine] * gate_ref[l]
                send_ref[mine, columns] = (total[other] * gate_ref[l]).astype(BF16)

    if streamed:
        resident = pl.BlockSpec((rows, half), lambda i: (0, 0))
        column = pl.BlockSpec((rows // 2, tile), lambda i: (0, i))
        specs = {
            "grid": (width // tile,),
            "in_specs": [SCALAR, SCALAR, resident, resident]
            + [pl.BlockSpec((2 * half, tile), lambda i: (0, i + first // tile))],
            "out_specs": [column, column],
            "compiler_params": params(44),
        }
    else:
        specs = {
            "in_specs": [SCALAR, SCALAR, INSIDE, INSIDE, INSIDE],
            "out_specs": [INSIDE, INSIDE],
            "compiler_params": params(),
        }
    return pl.pallas_call(
        kernel,
        out_shape=[
            jax.ShapeDtypeStruct((rows // 2, width), F32),
            jax.ShapeDtypeStruct((rows // 2, width), BF16),
        ],
        cost_estimate=pl.CostEstimate(
            flops=4 * rows * half * width,
            bytes_accessed=4 * rows * half + 3 * rows * width,
            transcendentals=0,
        ),
        **specs,
    )(places, gates, hidden, far, w_down)


def join(kept, arrived):
    def kernel(kept_ref, arrived_ref, out_ref):
        out_ref[...] = (kept_ref[...] + arrived_ref[...].astype(F32)).astype(BF16)

    size = kept.shape[0] * kept.shape[1]
    return pl.pallas_call(
        kernel,
        out_shape=jax.ShapeDtypeStruct(kept.shape, BF16),
        in_specs=[INSIDE, INSIDE],
        out_specs=INSIDE,
        cost_estimate=pl.CostEstimate(flops=size, bytes_accessed=8 * size, transcendentals=0),
        compiler_params=params(),
    )(kept, arrived)


def share_out(kept, arrived, near, places, lines, rows, capacity):
    width = kept.shape[1]

    def kernel(place_ref, kept_ref, arrived_ref, near_ref, *out_refs):
        for k in range(lines):
            mine = place_ref[2 * capacity + 2 * k]
            other = place_ref[2 * capacity + 2 * k + 1]
            start = pl.multiple_of(jnp.minimum(mine, capacity - 1) * rows, rows)
            value = kept_ref[pl.ds(start, rows), :] + arrived_ref[pl.ds(start, rows), :].astype(F32)
            value = jnp.where(mine < capacity, value, 0.0)
            start = pl.multiple_of(jnp.minimum(other, capacity - 1) * rows, rows)
            more = near_ref[pl.ds(start, rows), :].astype(F32)
            value = value + jnp.where(other < capacity, more, 0.0)
            out_refs[k][...] = value.astype(out_refs[k].dtype)

    size = rows * width
    kinds = [F32] + [BF16] * (lines - 1)
    return pl.pallas_call(
        kernel,
        out_shape=[jax.ShapeDtypeStruct((rows, width), kind) for kind in kinds],
        in_specs=[SCALAR, INSIDE, INSIDE, INSIDE],
        out_specs=[INSIDE] * lines,
        cost_estimate=pl.CostEstimate(
            flops=8 * size, bytes_accessed=(8 * capacity + 10) * size, transcendentals=0
        ),
        compiler_params=params(),
    )(places, kept, arrived, near)


def finish(groups, width):
    rows = groups[0][0].shape[0]
    count = len(groups[0])

    def kernel(*refs):
        out_ref, first = refs[-1], 0
        for j, group in enumerate(groups):
            part = refs[j * count : (j + 1) * count]
            total = part[0][...]
            for ref in part[1:]:
                total = total + ref[...].astype(F32)
            step = group[0].shape[1]
            out_ref[:, first : first + step] = total.astype(BF16)
            first += step

    size = rows * width
    return pl.pallas_call(
        kernel,
        out_shape=jax.ShapeDtypeStruct((rows, width), BF16),
        in_specs=[INSIDE] * (count * len(groups)),
        out_specs=INSIDE,
        cost_estimate=pl.CostEstimate(
            flops=count * size, bytes_accessed=(2 * count + 4) * size, transcendentals=0
        ),
        compiler_params=params(),
    )(*(a for group in groups for a in group))


def homed(tokens, w_gate, w_up, w_down, routes, gate_values):
    seq_count = lax.axis_size("seq")
    lines, pairs, halves = seq_count // 4, 2, 2
    capacity = 3 * routes.shape[0] // 8
    rows, width = tokens.shape

    flip_y = [(s, s ^ 2) for s in range(seq_count)]
    flip_x = [(s, s ^ 1) for s in range(seq_count)]
    swap = [(0, 1), (1, 0)]

    def along_z(k):
        return [(s, s ^ (4 * k)) for s in range(seq_count)]

    step = width // D_CHUNKS
    held = []
    for j in range(D_CHUNKS):
        chunk = tokens[:, j * step : (j + 1) * step]
        held.append([chunk] + [lax.ppermute(chunk, "seq", along_z(k)) for k in range(1, lines)])

    places, gates = tables(routes, gate_values, lines, pairs, halves, capacity)

    own = []
    for j in range(D_CHUNKS):
        leave = pick(held[j], places, capacity, capacity, rows)
        came = lax.ppermute(leave, "seq", flip_y)
        own.append(pick(held[j], places, 0, capacity, rows, came))
    mate = [lax.ppermute(a, "seq", flip_x) for a in own]
    far = [lax.ppermute(a, "tensor", swap) for a in own]
    mate_far = [lax.ppermute(a, "tensor", swap) for a in mate]

    state = ()
    size = D_CHUNKS // GROUPS
    for group in range(GROUPS):
        pieces = [
            (own[j], far[j], mate[j], mate_far[j]) for j in range(group * size, (group + 1) * size)
        ]
        state = gate_up(pieces, w_gate[0], w_up[0], places, group, 512, state)
    hidden = state
    hidden_far = lax.ppermute(hidden, "tensor", swap)

    step = width // C_CHUNKS
    kept, arrived = [], []
    for j in range(C_CHUNKS):
        keep, leave = down(hidden, hidden_far, w_down[0], places, gates, 256, j * step, step)
        kept.append(keep)
        arrived.append(lax.ppermute(leave, "seq", flip_x))
    results = []
    for j in range(C_CHUNKS):
        leave = join(kept[j], arrived[j])
        near = lax.ppermute(leave, "seq", flip_y)
        outgoing = share_out(kept[j], arrived[j], near, places, lines, rows, capacity)
        came = [lax.ppermute(outgoing[k], "seq", along_z(k)) for k in range(1, lines)]
        results.append([outgoing[0]] + came)
    return finish(results, width)


def solution(mesh):
    placed = (
        P("seq", "tensor"),
        P("seq", None, "tensor"),
        P("seq", None, "tensor"),
        P("seq", None, "tensor"),
        P(),
        P(),
    )
    seq_count, tensor_count = mesh.shape["seq"], mesh.shape["tensor"]
    shared_home = seq_count == 2 * E and tensor_count == 2

    def per_device(*arrays):
        return homed(*arrays) if shared_home else gathered(*arrays)

    return jax.shard_map(
        per_device, mesh=mesh, in_specs=placed, out_specs=P("seq", "tensor"), check_vma=False
    )
```
